256 devices in a mesh: row: 8 (over x, y_hi), col: 32 (over z, y_lo, core).
Axes of the slice: x: 4, y: 4 (y_hi: 2, y_lo: 2; y = y_hi * 2 + y_lo), z: 8, core: 2. Of those that a mesh axis runs over, the one named last changes fastest.
Arguments:
- left_panel: float32 [4096, 8192], P('col', 'row'), may hold values from -6 to 6
- right_panel: float32 [4096, 16384], P('row', 'col'), may hold values from -0.09375 to 0.09375
- arc_basis: float32 [4096, 256], replicated, as said below
- normal_block: float32 [8192, 16384], P('row', 'col'), may hold values from -6 to 6
Outputs:
- updated_block: float32 [8192, 16384], P('row', 'col')
- left_reduced: float32 [4096, 8192], P('col', 'row')
- right_reduced: float32 [4096, 16384], P('row', 'col')
The draws below stay inside these ranges and needn't reach their ends.
Inputs may be any that keep to these rules, and one draw needn't show every extreme that they name: arc_basis has orthonormal columns: arc_basis^T arc_basis equals the 256 x 256 identity within float32 rounding.
All inputs are finite; a program needn't handle non-finite values.
Results may differ from the reference program's by a relative error of at most 0.00005.
Values sent between devices are 32-bit elements; how exact they have to be, the bound alone decides.
No kernel may reach another device: no remote copies, remote signals or barrier semaphores. Data moves between devices by JAX's collectives and lax.ppermute only.
A program may use at most 128 MiB of HBM per device.

```python
import jax
import jax.numpy as jnp
from jax import lax

M = 4096
NL = 8192
NR = 16384
K = 256


def cholesky_pass(columns):
    gram = jnp.dot(columns.T, columns, precision=lax.Precision.HIGHEST, preferred_element_type=jnp.float32)
    factor = jnp.linalg.cholesky(gram)
    solved = jax.scipy.linalg.solve_triangular(factor, columns.T, lower=True)
    return solved.T


def draw_arc_basis(key, part):
    first = jax.random.fold_in(jax.random.fold_in(key, 7301), 0)
    raw = jax.random.normal(first, (M, K), jnp.float32)
    raw = raw * M ** (-0.5)
    return cholesky_pass(cholesky_pass(raw)).astype(jnp.float32)


def levels(key, shape, shards, smallest, largest):
    loudness = 1.0
    for dim, shards_of in shards:
        steps = jax.random.uniform(jax.random.fold_in(jax.random.fold_in(key, 6), dim), (shards_of,), jnp.float32, smallest / len(shards), largest / len(shards))
        loudness = loudness * jnp.repeat(jnp.exp(steps), shape[dim] // shards_of).reshape((-1,) + (1,) * (len(shape) - 1 - dim))
    return loudness


def normal_values(key, shape, scale, reach, cuts=(), dtype=jnp.bfloat16):
    drawn = jax.random.normal(key, shape, jnp.float32) * scale
    if len(cuts) > 0:
        drawn = levels(key, shape, cuts, -0.22, 0.18) * drawn
    return jnp.clip(drawn, min=-reach, max=reach).astype(dtype)


def setup_inputs(seed: int = 0) -> dict:
    keys = jax.random.split(jax.random.key(seed), 5)
    return {
        "left_panel": normal_values(keys[0], (M, NL), 1.0, 6.0, ((0, 32), (1, 8)), jnp.float32),
        "right_panel": normal_values(keys[1], (M, NR), M ** -0.5, 0.09375, ((0, 8), (1, 32)), jnp.float32),
        "arc_basis": draw_arc_basis(jax.random.fold_in(keys[4], 71), 0),
        "normal_block": normal_values(keys[3], (NL, NR), 1.0, 6.0, ((0, 8), (1, 32)), jnp.float32),
    }


def reference(left_panel, right_panel, arc_basis, normal_block):
    highest = lax.Precision.HIGHEST
    left_coef = jnp.dot(arc_basis.T.astype(jnp.float32), left_panel.astype(jnp.float32), precision=highest, preferred_element_type=jnp.float32)
    right_coef = jnp.dot(arc_basis.T.astype(jnp.float32), right_panel.astype(jnp.float32), precision=highest, preferred_element_type=jnp.float32)
    left_reduced = left_panel - jnp.dot(arc_basis.astype(jnp.float32), left_coef.astype(jnp.float32), precision=highest, preferred_element_type=jnp.float32)
    right_reduced = right_panel - jnp.dot(arc_basis.astype(jnp.float32), right_coef.astype(jnp.float32), precision=highest, preferred_element_type=jnp.float32)
    updated_block = normal_block + jnp.dot(left_reduced.T.astype(jnp.float32), right_reduced.astype(jnp.float32), precision=highest, preferred_element_type=jnp.float32)
    return (updated_block, left_reduced, right_reduced)
```

```python
import jax
import jax.numpy as jnp
from jax import lax
from jax.sharding import Mesh
from jax.sharding import PartitionSpec as P

AXES = ("x", "y_hi", "z", "y_lo", "core")
ROW = ("x", "y_hi")
COL = ("z", "y_lo", "core")
FIRST = (((0,), (0,)), ((), ()))
PLAIN = (((1,), (0,)), ((), ()))


def product(first, second, dims=FIRST):
    return lax.dot_general(
        first, second, dims, precision=lax.Precision.HIGH, preferred_element_type=jnp.float32
    )


def swap(block, axis):
    return lax.ppermute(block, axis, [(0, 1), (1, 0)])


def lane_step(block, axis, size):
    pairs = []
    for place in range(size):
        pairs.append((place * 2, (place + 1) % size * 2))
        pairs.append((place * 2 + 1, (place - 1) % size * 2 + 1))
    return lax.ppermute(block, (axis, "core"), pairs)


def local(left_panel, right_panel, arc_basis, normal_block):
    x, y_hi, z, y_lo, core = (lax.axis_index(name) for name in AXES)
    left_rows, right_rows = left_panel.shape[0], right_panel.shape[0]
    half = left_panel.shape[1] // 2
    sizes = {name: lax.axis_size(name) for name in AXES}
    up = 1 - 2 * core
    row_index = x * sizes["y_hi"] + y_hi
    col_index = (z * sizes["y_lo"] + y_lo) * 2 + core

    left_whole = lax.all_gather(left_panel, COL, axis=0, tiled=True)

    mine, other = right_panel, swap(right_panel, "y_hi")
    right_whole = jnp.zeros((arc_basis.shape[0], right_panel.shape[1]), jnp.float32)
    for step in range(sizes["x"]):
        place = lax.rem(x - up * step + sizes["x"], sizes["x"]) * sizes["y_hi"]
        for block, hi in ((mine, y_hi), (other, 1 - y_hi)):
            right_whole = lax.dynamic_update_slice_in_dim(
                right_whole, block, (place + hi) * right_rows, 0
            )
        if step < sizes["x"] - 1:
            mine = lane_step(mine, "x", sizes["x"])
            other = lane_step(other, "x", sizes["x"])

    right_coef = product(arc_basis, right_whole)
    right_kept = right_whole - product(arc_basis, right_coef, PLAIN)
    right_reduced = lax.dynamic_slice_in_dim(right_kept, row_index * right_rows, right_rows, 0)

    own_half = lax.dynamic_slice_in_dim(left_whole, core * half, half, 1)
    coef_half = product(arc_basis, own_half)
    coef_other = swap(coef_half, "core")
    basis_own = lax.dynamic_slice_in_dim(arc_basis, col_index * left_rows, left_rows, 0)
    near = product(basis_own, coef_half, PLAIN)
    far = product(basis_own, coef_other, PLAIN)
    fitted = jnp.where(
        core == 0, jnp.concatenate([near, far], 1), jnp.concatenate([far, near], 1)
    )
    left_reduced = left_panel - fitted
    updated_block = normal_block + product(left_whole, right_kept)
    return (updated_block, left_reduced, right_reduced)


def solution(mesh):
    split = Mesh(mesh.devices.reshape(4, 2, 8, 2, 2), AXES)
    in_specs = (P(COL, ROW), P(ROW, COL), P(), P(ROW, COL))
    out_specs = (P(ROW, COL), P(COL, ROW), P(ROW, COL))
    return jax.shard_map(local, mesh=split, in_specs=in_specs, out_specs=out_specs, check_vma=False)
```

```python
import functools

import jax
import jax.numpy as jnp
from jax import lax
from jax.experimental import pallas as pl
from jax.experimental.pallas import tpu as pltpu
from jax.sharding import Mesh
from jax.sharding import PartitionSpec as P

AXES = ("x", "y_hi", "z", "y_lo", "core")
ROW = ("x", "y_hi")
COL = ("z", "y_lo", "core")
VMEM = pl.BlockSpec(memory_space=pltpu.VMEM)
SMEM = pl.BlockSpec(memory_space=pltpu.SMEM)
F32, BF16 = jnp.float32, jnp.bfloat16
FIRST = (((0,), (0,)), ((), ()))
PLAIN = (((1,), (0,)), ((), ()))
LINES = 128
PAIR, SLAB = 2 * LINES, 4 * LINES


def product(first, second, dims):
    return lax.dot_general(
        first, second, dims, precision=lax.Precision.HIGH, preferred_element_type=F32
    )


def swap(block, axis):
    return lax.ppermute(block, axis, [(0, 1), (1, 0)])


def lane_step(block, axis, size):
    pairs = []
    for place in range(size):
        pairs.append((place * 2, (place + 1) % size * 2))
        pairs.append((place * 2 + 1, (place - 1) % size * 2 + 1))
    return lax.ppermute(block, (axis, "core"), pairs)


def later(value, *arrived):
    return lax.optimization_barrier((value, *arrived))[0]


def halves(value):
    high = value.astype(BF16)
    return high, (value - high.astype(F32)).astype(BF16)


def dot(first, second):
    return jnp.dot(first, second, preferred_element_type=F32)


def rows_at(place):
    return pl.ds(pl.multiple_of(place * LINES, LINES), LINES)


def spread(blocks, wide):
    for j, ref in enumerate(blocks):
        for k, value in enumerate(halves(ref[...])):
            at = (k * len(blocks) + j) * LINES
            wide[:, at : at + LINES] = value


def coef_body(steps, places, *refs):
    basis, coef, wide = refs[2 * steps :]
    for step in range(steps):
        rows = [basis[rows_at(places[step * 4 + j]), :] for j in range(2)]
        high, low = halves(jnp.concatenate(rows, 0))
        spread(refs[2 * step : 2 * step + 2], wide)
        top, bottom = wide[:, :PAIR], wide[:, PAIR:]
        value = dot(
            jnp.concatenate([top, bottom, top], 1), jnp.concatenate([high, high, low], 0)
        )
        coef[...] = coef[...] + value if step else value


def main_body(steps, lines, places, *refs):
    right_near, right_far, before, out, wide = refs[4 * steps :]
    for step in range(steps):
        pieces = []
        for j in range(4):
            rows = rows_at(places[step * 4 + j])
            pieces.append(
                jnp.where(lines[step * 4 + j] == 0, right_near[rows, :], right_far[rows, :])
            )
        high, low = halves(jnp.concatenate(pieces, 0))
        tall = jnp.concatenate([high, high, low], 0)
        spread(refs[4 * step : 4 * step + 4], wide)
        top, bottom = wide[:, :SLAB], wide[:, SLAB:]
        both = jnp.concatenate([top, bottom, top], 1)
        for at in range(0, out.shape[1], 256):
            tile = slice(at, at + 256)
            out[:, tile] = (out if step else before)[:, tile] + dot(both, tall[:, tile])


def left_body(left, basis, coef, other, out):
    high, low = halves(basis[...])
    top, bottom = halves(coef[...] + other[...])
    fitted = lax.dot_general(
        jnp.concatenate([high, low, high], 1),
        jnp.concatenate([top, top, bottom], 1),
        (((1,), (1,)), ((), ())),
        preferred_element_type=F32,
    )
    out[...] = left[...] - fitted


def kernel(body, name, outs, specs, limit, flops, moved, columns=0):
    return pl.pallas_call(
        body,
        out_shape=outs,
        in_specs=specs,
        out_specs=[VMEM] * len(outs),
        scratch_shapes=[pltpu.VMEM((outs[0].shape[0], columns), BF16)] if columns else [],
        name=name,
        cost_estimate=pl.CostEstimate(flops=flops, bytes_accessed=moved, transcendentals=0),
        compiler_params=pltpu.CompilerParams(vmem_limit_bytes=limit << 20),
    )


def local(left_panel, right_panel, arc_basis, normal_block):
    x, y_hi, z, y_lo, core = (lax.axis_index(name) for name in AXES)
    nx, nz = lax.axis_size("x"), lax.axis_size("z")
    observations, arcs = arc_basis.shape
    width, depth = left_panel.shape[1], right_panel.shape[1]
    count = right_panel.shape[0]
    line = nx * count
    up = 1 - 2 * core
    shape = jax.ShapeDtypeStruct

    own = [left_panel.T]
    beside = [swap(own[0], "y_lo")]
    other = swap(later(right_panel, beside[0]), "y_hi")
    left_places, right_places, lines = [], [], []
    for step in range(nz):
        for lane, sign in ((core, up), (1 - core, -up)):
            from_z = lax.rem(z - sign * step + nz, nz)
            for lo in (y_lo, 1 - y_lo):
                spot = lo * 2 + lane
                left_places.append((from_z * 4 + spot).astype(jnp.int32))
                hops = lax.rem(up * (x - lax.div(from_z, 2)) + nx, nx)
                right_places.append((hops * 4 + spot).astype(jnp.int32))
                lines.append((lax.rem(from_z, 2) != y_hi).astype(jnp.int32))

    def left_coef(first, last):
        steps = last - first
        return kernel(
            functools.partial(coef_body, steps), "left_coef", [shape((width, arcs), F32)],
            [SMEM] + [VMEM] * (2 * steps + 1), 14, 6 * width * steps * PAIR * arcs,
            steps * PAIR * (width + arcs) * 4, 2 * PAIR,
        )(jnp.stack(left_places[first * 4 : last * 4]),
          *[side[k] for k in range(first, last) for side in (own, beside)], arc_basis)[0]

    def basis_line(hi):
        slabs = [lax.rem(x - up * hop + nx, nx) * 2 + hi for hop in range(nx)]
        return jnp.concatenate(
            [lax.dynamic_slice_in_dim(arc_basis, slab * count, count, 0) for slab in slabs], 0
        )

    basis_near, basis_far = basis_line(y_hi), basis_line(1 - y_hi)
    mine, others, traded = [right_panel], [], []
    for step in range(nz):
        own_gate = list(traded[step - 2]) if step >= 2 else []
        beside_gate = []
        if step < nx - 1:
            mine.append(lane_step(later(mine[step], own[step]) if step else mine[0], "x", nx))
        if step >= 3 and step - 3 < nx:
            other = later(other, own[step])
            others.append(other)
            if step > 3:
                beside_gate.append(other)
            if step - 3 < nx - 1:
                other = lane_step(other, "x", nx)
        if step == 5:
            right_near = jnp.concatenate(mine, 0)
            beside_gate.append(right_near[:8, :128])
        if step == 6:
            early_coef = left_coef(0, 5)
            own_gate.append(early_coef)
            right_coef = product(basis_near, right_near, FIRST)
            beside_gate.append(right_coef)
        if step < nz - 1:
            own.append(lane_step(later(own[step], *own_gate), "z", nz))
            beside.append(lane_step(later(beside[step], *beside_gate), "z", nz))
        traded.append((swap(own[step], "core"), swap(beside[step], "core")))

    right_far = jnp.concatenate(others, 0)
    right_coef = right_coef + product(basis_far, right_far, FIRST)
    kept_near = right_near - product(basis_near, right_coef, PLAIN)
    kept_far = right_far - product(basis_far, right_coef, PLAIN)
    coef = early_coef + left_coef(5, nz)

    updated_block = normal_block
    for first, last in ((0, 6), (6, nz)):
        steps = last - first
        words = [jnp.stack(w[first * 4 : last * 4]) for w in (lines, right_places)]
        (updated_block,) = kernel(
            functools.partial(main_body, steps), "block_update", [shape((width, depth), F32)],
            [SMEM] * 2 + [VMEM] * (4 * steps + 3), 16, 6 * width * steps * SLAB * depth,
            steps * SLAB * (width + depth) * 4, 2 * SLAB,
        )(*words, *[block for k in range(first, last) for block in (own[k], beside[k], *traded[k])],
          kept_near, kept_far, updated_block)

    right_reduced = kept_near[:count]
    col_index = (z * 2 + y_lo) * 2 + core
    basis_left = lax.dynamic_slice_in_dim(arc_basis, col_index * LINES, LINES, 0)
    (left_reduced,) = kernel(
        left_body, "left_reduce", [shape(left_panel.shape, F32)], [VMEM] * 4, 8,
        6 * LINES * arcs * width, LINES * width * 8,
    )(left_panel, basis_left, coef, swap(coef, "core"))
    return (updated_block, left_reduced, right_reduced)


def solution(mesh):
    split = Mesh(mesh.devices.reshape(4, 2, 8, 2, 2), AXES)
    in_specs = (P(COL, ROW), P(ROW, COL), P(), P(ROW, COL))
    out_specs = (P(ROW, COL), P(COL, ROW), P(ROW, COL))
    return jax.shard_map(local, mesh=split, in_specs=in_specs, out_specs=out_specs, check_vma=False)
```

```python
import functools

import jax
import jax.numpy as jnp
from jax import lax
from jax.experimental import pallas as pl
from jax.experimental.pallas import tpu as pltpu
from jax.sharding import Mesh
from jax.sharding import PartitionSpec as P

AXES = ("x", "y_hi", "z", "y_lo", "core")
ROW = ("x", "y_hi")
COL = ("z", "y_lo", "core")
VMEM = pl.BlockSpec(memory_space=pltpu.VMEM)
SMEM = pl.BlockSpec(memory_space=pltpu.SMEM)
F32, BF16 = jnp.float32, jnp.bfloat16
FIRST = (((0,), (0,)), ((), ()))
PLAIN = (((1,), (0,)), ((), ()))
LINES = 128
PAIR, SLAB = 2 * LINES, 4 * LINES


def product(first, second, dims):
    return lax.dot_general(
        first, second, dims, precision=lax.Precision.HIGH, preferred_element_type=F32
    )


def swap(block, axis):
    return lax.ppermute(block, axis, [(0, 1), (1, 0)])


def lane_step(block, axis, size):
    pairs = []
    for place in range(size):
        pairs.append((place * 2, (place + 1) % size * 2))
        pairs.append((place * 2 + 1, (place - 1) % size * 2 + 1))
    return lax.ppermute(block, (axis, "core"), pairs)


def later(value, *arrived):
    return lax.optimization_barrier((value, *arrived))[0]


def halves(value):
    high = value.astype(BF16)
    return high, (value - high.astype(F32)).astype(BF16)


def dot(first, second):
    return jnp.dot(first, second, preferred_element_type=F32)


def rows_at(place):
    return pl.ds(pl.multiple_of(place * LINES, LINES), LINES)


def spread(blocks, wide):
    for j, ref in enumerate(blocks):
        for k, value in enumerate(halves(ref[...])):
            at = (k * len(blocks) + j) * LINES
            wide[:, at : at + LINES] = value


def coef_body(steps, places, *refs):
    basis, coef, wide = refs[2 * steps :]
    for step in range(steps):
        rows = [basis[rows_at(places[step * 4 + j]), :] for j in range(2)]
        high, low = halves(jnp.concatenate(rows, 0))
        spread(refs[2 * step : 2 * step + 2], wide)
        top, bottom = wide[:, :PAIR], wide[:, PAIR:]
        value = dot(
            jnp.concatenate([top, bottom, top], 1), jnp.concatenate([high, high, low], 0)
        )
        coef[...] = coef[...] + value if step else value


def main_body(steps, lines, places, *refs):
    right_near, right_far, before, out, wide = refs[4 * steps :]
    for step in range(steps):
        pieces = []
        for j in range(4):
            rows = rows_at(places[step * 4 + j])
            pieces.append(
                jnp.where(lines[step * 4 + j] == 0, right_near[rows, :], right_far[rows, :])
            )
        high, low = halves(jnp.concatenate(pieces, 0))
        tall = jnp.concatenate([high, high, low], 0)
        spread(refs[4 * step : 4 * step + 4], wide)
        top, bottom = wide[:, :SLAB], wide[:, SLAB:]
        both = jnp.concatenate([top, bottom, top], 1)
        for at in range(0, out.shape[1], 256):
            tile = slice(at, at + 256)
            out[:, tile] = (out if step else before)[:, tile] + dot(both, tall[:, tile])


def left_body(left, basis, coef, other, out):
    high, low = halves(basis[...])
    top, bottom = halves(coef[...] + other[...])
    fitted = lax.dot_general(
        jnp.concatenate([high, low, high], 1),
        jnp.concatenate([top, top, bottom], 1),
        (((1,), (1,)), ((), ())),
        preferred_element_type=F32,
    )
    out[...] = left[...] - fitted


def kernel(body, name, outs, specs, limit, flops, moved, columns=0):
    return pl.pallas_call(
        body,
        out_shape=outs,
        in_specs=specs,
        out_specs=[VMEM] * len(outs),
        scratch_shapes=[pltpu.VMEM((outs[0].shape[0], columns), BF16)] if columns else [],
        name=name,
        cost_estimate=pl.CostEstimate(flops=flops, bytes_accessed=moved, transcendentals=0),
        compiler_params=pltpu.CompilerParams(vmem_limit_bytes=limit << 20),
    )


def local(left_panel, right_panel, arc_basis, normal_block):
    x, y_hi, z, y_lo, core = (lax.axis_index(name) for name in AXES)
    nx, nz = lax.axis_size("x"), lax.axis_size("z")
    observations, arcs = arc_basis.shape
    width, depth = left_panel.shape[1], right_panel.shape[1]
    count = right_panel.shape[0]
    line = nx * count
    up = 1 - 2 * core
    shape = jax.ShapeDtypeStruct

    own = [left_panel.T]
    beside = [swap(own[0], "y_lo")]
    other = swap(later(right_panel, beside[0]), "y_hi")
    left_places, right_places, lines = [], [], []
    for step in range(nz):
        for lane, sign in ((core, up), (1 - core, -up)):
            from_z = lax.rem(z - sign * step + nz, nz)
            for lo in (y_lo, 1 - y_lo):
                spot = lo * 2 + lane
                left_places.append((from_z * 4 + spot).astype(jnp.int32))
                hops = lax.rem(up * (x - lax.div(from_z, 2)) + nx, nx)
                right_places.append((hops * 4 + spot).astype(jnp.int32))
                lines.append((lax.rem(from_z, 2) != y_hi).astype(jnp.int32))

    def left_coef(first, last):
        steps = last - first
        return kernel(
            functools.partial(coef_body, steps), "left_coef", [shape((width, arcs), F32)],
            [SMEM] + [VMEM] * (2 * steps + 1), 14, 6 * width * steps * PAIR * arcs,
            steps * PAIR * (width + arcs) * 4, 2 * PAIR,
        )(jnp.stack(left_places[first * 4 : last * 4]),
          *[side[k] for k in range(first, last) for side in (own, beside)], arc_basis)[0]

    def basis_line(hi):
        slabs = [lax.rem(x - up * hop + nx, nx) * 2 + hi for hop in range(nx)]
        return jnp.concatenate(
            [lax.dynamic_slice_in_dim(arc_basis, slab * count, count, 0) for slab in slabs], 0
        )

    basis_near, basis_far = basis_line(y_hi), basis_line(1 - y_hi)
    mine, others, traded = [right_panel], [], []
    for step in range(nz):
        own_gate = list(traded[step - 2]) if step >= 2 else []
        beside_gate = []
        if step < nx - 1:
            mine.append(lane_step(later(mine[step], own[step]) if step else mine[0], "x", nx))
        if step >= 3 and step - 3 < nx:
            other = later(other, own[step])
            others.append(other)
            if step > 3:
                beside_gate.append(other)
            if step - 3 < nx - 1:
                other = lane_step(other, "x", nx)
        if step == 5:
            right_near = jnp.concatenate(mine, 0)
            beside_gate.append(right_near[:8, :128])
        if step == 6:
            early_coef = left_coef(0, 5)
            own_gate.append(early_coef)
            right_coef = product(basis_near, right_near, FIRST)
            beside_gate.append(right_coef)
        if step < nz - 1:
            own.append(lane_step(later(own[step], *own_gate), "z", nz))
            beside.append(lane_step(later(beside[step], *beside_gate), "z", nz))
        traded.append((swap(own[step], "core"), swap(beside[step], "core")))

    right_far = jnp.concatenate(others, 0)
    right_coef = right_coef + product(basis_far, right_far, FIRST)
    kept_near = right_near - product(basis_near, right_coef, PLAIN)
    kept_far = right_far - product(basis_far, right_coef, PLAIN)
    coef = early_coef + left_coef(5, nz)

    updated_block = normal_block
    for first, last in ((0, nz),):
        steps = last - first
        words = [jnp.stack(w[first * 4 : last * 4]) for w in (lines, right_places)]
        (updated_block,) = kernel(
            functools.partial(main_body, steps), "block_update", [shape((width, depth), F32)],
            [SMEM] * 2 + [VMEM] * (4 * steps + 3), 16, 6 * width * steps * SLAB * depth,
            steps * SLAB * (width + depth) * 4, 2 * SLAB,
        )(*words, *[block for k in range(first, last) for block in (own[k], beside[k], *traded[k])],
          kept_near, kept_far, updated_block)

    right_reduced = kept_near[:count]
    col_index = (z * 2 + y_lo) * 2 + core
    basis_left = lax.dynamic_slice_in_dim(arc_basis, col_index * LINES, LINES, 0)
    (left_reduced,) = kernel(
        left_body, "left_reduce", [shape(left_panel.shape, F32)], [VMEM] * 4, 8,
        6 * LINES * arcs * width, LINES * width * 8,
    )(left_panel, basis_left, coef, swap(coef, "core"))
    return (updated_block, left_reduced, right_reduced)


def solution(mesh):
    split = Mesh(mesh.devices.reshape(4, 2, 8, 2, 2), AXES)
    in_specs = (P(COL, ROW), P(ROW, COL), P(), P(ROW, COL))
    out_specs = (P(ROW, COL), P(COL, ROW), P(ROW, COL))
    return jax.shard_map(local, mesh=split, in_specs=in_specs, out_specs=out_specs, check_vma=False)
```

```python
import functools

import jax
import jax.numpy as jnp
from jax import lax
from jax.experimental import pallas as pl
from jax.experimental.pallas import tpu as pltpu
from jax.sharding import Mesh
from jax.sharding import PartitionSpec as P

AXES = ("x", "y_hi", "z", "y_lo", "core")
ROW = ("x", "y_hi")
COL = ("z", "y_lo", "core")
VMEM = pl.BlockSpec(memory_space=pltpu.VMEM)
SMEM = pl.BlockSpec(memory_space=pltpu.SMEM)
F32, BF16 = jnp.float32, jnp.bfloat16
FIRST = (((0,), (0,)), ((), ()))
PLAIN = (((1,), (0,)), ((), ()))
LINES = 128
PAIR, SLAB = 2 * LINES, 4 * LINES


def product(first, second, dims):
    return lax.dot_general(
        first, second, dims, precision=lax.Precision.HIGH, preferred_element_type=F32
    )


def swap(block, axis):
    return lax.ppermute(block, axis, [(0, 1), (1, 0)])


def lane_step(block, axis, size):
    pairs = []
    for place in range(size):
        pairs.append((place * 2, (place + 1) % size * 2))
        pairs.append((place * 2 + 1, (place - 1) % size * 2 + 1))
    return lax.ppermute(block, (axis, "core"), pairs)


def later(value, *arrived):
    return lax.optimization_barrier((value, *arrived))[0]


def halves(value):
    high = value.astype(BF16)
    return high, (value - high.astype(F32)).astype(BF16)


def dot(first, second):
    return jnp.dot(first, second, preferred_element_type=F32)


def rows_at(place):
    return pl.ds(pl.multiple_of(place * LINES, LINES), LINES)


def spread(blocks, wide):
    for j, ref in enumerate(blocks):
        for k, value in enumerate(halves(ref[...])):
            at = (k * len(blocks) + j) * LINES
            wide[:, at : at + LINES] = value


def coef_body(steps, places, *refs):
    basis, coef, wide = refs[2 * steps :]
    for step in range(steps):
        rows = [basis[rows_at(places[step * 4 + j]), :] for j in range(2)]
        high, low = halves(jnp.concatenate(rows, 0))
        spread(refs[2 * step : 2 * step + 2], wide)
        top, bottom = wide[:, :PAIR], wide[:, PAIR:]
        value = dot(
            jnp.concatenate([top, bottom, top], 1), jnp.concatenate([high, high, low], 0)
        )
        coef[...] = coef[...] + value if step else value


def main_body(steps, lines, places, *refs):
    right_near, right_far, before, out, wide = refs[4 * steps :]
    for step in range(steps):
        pieces = []
        for j in range(4):
            rows = rows_at(places[step * 4 + j])
            pieces.append(
                jnp.where(lines[step * 4 + j] == 0, right_near[rows, :], right_far[rows, :])
            )
        high, low = halves(jnp.concatenate(pieces, 0))
        tall = jnp.concatenate([high, high, low], 0)
        spread(refs[4 * step : 4 * step + 4], wide)
        top, bottom = wide[:, :SLAB], wide[:, SLAB:]
        both = jnp.concatenate([top, bottom, top], 1)
        for at in range(0, out.shape[1], 256):
            tile = slice(at, at + 256)
            out[:, tile] = (out if step else before)[:, tile] + dot(both, tall[:, tile])


def left_body(left, basis, coef, other, out):
    high, low = halves(basis[...])
    top, bottom = halves(coef[...] + other[...])
    fitted = lax.dot_general(
        jnp.concatenate([high, low, high], 1),
        jnp.concatenate([top, top, bottom], 1),
        (((1,), (1,)), ((), ())),
        preferred_element_type=F32,
    )
    out[...] = left[...] - fitted


def kernel(body, name, outs, specs, limit, flops, moved, columns=0):
    return pl.pallas_call(
        body,
        out_shape=outs,
        in_specs=specs,
        out_specs=[VMEM] * len(outs),
        scratch_shapes=[pltpu.VMEM((outs[0].shape[0], columns), BF16)] if columns else [],
        name=name,
        cost_estimate=pl.CostEstimate(flops=flops, bytes_accessed=moved, transcendentals=0),
        compiler_params=pltpu.CompilerParams(vmem_limit_bytes=limit << 20),
    )


def local(left_panel, right_panel, arc_basis, normal_block):
    x, y_hi, z, y_lo, core = (lax.axis_index(name) for name in AXES)
    nx, nz = lax.axis_size("x"), lax.axis_size("z")
    observations, arcs = arc_basis.shape
    width, depth = left_panel.shape[1], right_panel.shape[1]
    count = right_panel.shape[0]
    line = nx * count
    up = 1 - 2 * core
    shape = jax.ShapeDtypeStruct

    own = [left_panel.T]
    beside = [swap(own[0], "y_lo")]
    other = swap(later(right_panel, beside[0]), "y_hi")
    left_places, right_places, lines = [], [], []
    for step in range(nz):
        for lane, sign in ((core, up), (1 - core, -up)):
            from_z = lax.rem(z - sign * step + nz, nz)
            for lo in (y_lo, 1 - y_lo):
                spot = lo * 2 + lane
                left_places.append((from_z * 4 + spot).astype(jnp.int32))
                hops = lax.rem(up * (x - lax.div(from_z, 2)) + nx, nx)
                right_places.append((hops * 4 + spot).astype(jnp.int32))
                lines.append((lax.rem(from_z, 2) != y_hi).astype(jnp.int32))

    def left_coef(first, last):
        steps = last - first
        return kernel(
            functools.partial(coef_body, steps), "left_coef", [shape((width, arcs), F32)],
            [SMEM] + [VMEM] * (2 * steps + 1), 14, 6 * width * steps * PAIR * arcs,
            steps * PAIR * (width + arcs) * 4, 2 * PAIR,
        )(jnp.stack(left_places[first * 4 : last * 4]),
          *[side[k] for k in range(first, last) for side in (own, beside)], arc_basis)[0]

    def basis_line(hi):
        slabs = [lax.rem(x - up * hop + nx, nx) * 2 + hi for hop in range(nx)]
        return jnp.concatenate(
            [lax.dynamic_slice_in_dim(arc_basis, slab * count, count, 0) for slab in slabs], 0
        )

    basis_near, basis_far = basis_line(y_hi), basis_line(1 - y_hi)
    mine, others, traded = [right_panel], [], []
    for step in range(nz):
        own_gate = list(traded[step - 2]) if step >= 2 else []
        beside_gate = []
        if step < nx - 1:
            mine.append(lane_step(later(mine[step], own[step]) if step else mine[0], "x", nx))
        if step >= 3 and step - 3 < nx:
            other = later(other, own[step])
            others.append(other)
            if step > 3:
                beside_gate.append(other)
            if step - 3 < nx - 1:
                other = lane_step(other, "x", nx)
        if step == 5:
            right_near = jnp.concatenate(mine, 0)
            beside_gate.append(right_near[:8, :128])
        if step == 6:
            early_coef = left_coef(0, 5)
            right_coef = product(basis_near, right_near, FIRST)
            beside_gate.append(right_coef)
        if step < nz - 1:
            own.append(lane_step(later(own[step], *own_gate), "z", nz))
            beside.append(lane_step(later(beside[step], *beside_gate), "z", nz))
        traded.append((swap(own[step], "core"), swap(beside[step], "core")))

    right_far = jnp.concatenate(others, 0)
    right_coef = right_coef + product(basis_far, right_far, FIRST)
    kept_near = right_near - product(basis_near, right_coef, PLAIN)
    kept_far = right_far - product(basis_far, right_coef, PLAIN)
    coef = early_coef + left_coef(5, nz)

    updated_block = normal_block
    for first, last in ((0, nz),):
        steps = last - first
        words = [jnp.stack(w[first * 4 : last * 4]) for w in (lines, right_places)]
        (updated_block,) = kernel(
            functools.partial(main_body, steps), "block_update", [shape((width, depth), F32)],
            [SMEM] * 2 + [VMEM] * (4 * steps + 3), 16, 6 * width * steps * SLAB * depth,
            steps * SLAB * (width + depth) * 4, 2 * SLAB,
        )(*words, *[block for k in range(first, last) for block in (own[k], beside[k], *traded[k])],
          kept_near, kept_far, updated_block)

    right_reduced = kept_near[:count]
    col_index = (z * 2 + y_lo) * 2 + core
    basis_left = lax.dynamic_slice_in_dim(arc_basis, col_index * LINES, LINES, 0)
    (left_reduced,) = kernel(
        left_body, "left_reduce", [shape(left_panel.shape, F32)], [VMEM] * 4, 8,
        6 * LINES * arcs * width, LINES * width * 8,
    )(left_panel, basis_left, coef, swap(coef, "core"))
    return (updated_block, left_reduced, right_reduced)


def solution(mesh):
    split = Mesh(mesh.devices.reshape(4, 2, 8, 2, 2), AXES)
    in_specs = (P(COL, ROW), P(ROW, COL), P(), P(ROW, COL))
    out_specs = (P(ROW, COL), P(COL, ROW), P(ROW, COL))
    return jax.shard_map(local, mesh=split, in_specs=in_specs, out_specs=out_specs, check_vma=False)
```
